32 devices in a mesh: sample: 2 (over y), harm: 16 (over z, x, core).
Axes of the slice: x: 2, y: 2, z: 4, core: 2. Of those that a mesh axis runs over, the one named last changes fastest.
Arguments:
- inputs: bfloat16 [128, 64, 512], P('sample', 'harm'), parts along dimension 0, may hold values from -6 to 6
- col_list: int32 [128], P('sample'), parts along dimension 0, may hold values from 0 to 63, each once
- row_list: int32 [128], P('sample'), parts along dimension 0, may hold values from 0 to 63, each once
- gain_attn: float32 [512], replicated, may hold values from 0.25 to 1.75
- w_qkv: bfloat16 [512, 1536], replicated
- w_out: bfloat16 [512, 512], replicated, may hold values from -0.25 to 0.25
- gain_ffn: float32 [512], replicated, may hold values from 0.25 to 1.75
- w_gate: bfloat16 [512, 1024], P('harm'), may hold values from -0.25 to 0.25
- w_up: bfloat16 [512, 1024], P('harm'), may hold values from -0.25 to 0.25
- w_down: bfloat16 [1024, 512], P('harm'), may hold values from -0.1875 to 0.1875
Outputs:
- result: bfloat16 [64, 128, 512], P('harm', 'sample'), parts along dimension 1
The draws below stay inside these ranges and needn't reach their ends.
There are 2 independent parts, one for each index of `sample`. The reference program is written for one: setup_inputs(seed, part) draws one part's arguments, and reference() takes and returns one part's arrays. A program takes and returns all parts, laid end to end along the dimension named above; an argument that names none is the same for every part. Nothing has to cross between parts.
Inputs may be any that keep to these rules, and one draw needn't show every extreme that they name: col_list names every order m of 0 to 63 exactly once. row_list names every degree ell of 0 to 63 exactly once.
All inputs are finite; a program needn't handle non-finite values.
Results may differ from the reference program's by a relative error of at most 0.0073.
Values may be sent and summed in bfloat16 or wider, within the bound.
A program may use at most 64 MiB of HBM per device.

```python
import jax
import jax.numpy as jnp
from jax import lax

D = 512
HEADS = 8
FF = 1024
WIN = 256
LMAX = 64


def draw_w_qkv(key, part):
    first = jax.random.fold_in(key, 0)
    base = jax.random.normal(first, (D, 3 * D), jnp.float32) * (2.0 / D) ** 0.5
    return base.astype(jnp.bfloat16)


def shard_levels(rng, extent, shards, least, high):
    def one(position, shards_of):
        draws = jax.random.uniform(jax.random.fold_in(jax.random.fold_in(rng, 6), position), (shards_of,), jnp.float32, least / len(shards), high / len(shards))
        return jnp.repeat(jnp.exp(draws), extent[position] // shards_of).reshape((-1,) + (1,) * (len(extent) - position - 1))

    factor_of = one(*shards[0])
    for cut in shards[1:]:
        factor_of = factor_of * one(*cut)
    return factor_of


def centred(key, shape, width, most, pieces=(), kind=jnp.bfloat16):
    values = jax.random.normal(key, shape, jnp.float32) * width
    if len(pieces) > 0:
        values = shard_levels(key, shape, pieces, -0.22, 0.18) * values
    return jnp.clip(values, min=-most, max=most).astype(kind)


def setup_inputs(seed: int = 0, part: int = 0) -> dict:
    streams_of = jax.random.split(jax.random.key(seed), 11)
    part_keys = jax.random.split(jax.random.fold_in(streams_of[10], part), 11)
    inputs = centred(part_keys[0], (LMAX, LMAX, D), 1.0, 6.0, ((1, 16),))
    col_list = jax.random.permutation(part_keys[1], LMAX).astype(jnp.int32)
    row_list = jax.random.permutation(part_keys[2], LMAX).astype(jnp.int32)
    gain_attn = jnp.clip(1.0 + 0.15 * jax.random.normal(streams_of[3], (D,), jnp.float32), 0.25, 1.75)
    w_qkv = draw_w_qkv(jax.random.fold_in(streams_of[10], 71), part)
    w_out = centred(streams_of[5], (D, D), D ** -0.5, 0.25)
    gain_ffn = jnp.clip(1.0 + 0.15 * jax.random.normal(streams_of[6], (D,), jnp.float32), 0.25, 1.75)
    w_gate = centred(streams_of[7], (D, FF), D ** -0.5, 0.25, ((0, 16),))
    w_up = centred(streams_of[8], (D, FF), D ** -0.5, 0.25, ((0, 16),))
    w_down = centred(streams_of[9], (FF, D), FF ** -0.5, 0.1875, ((0, 16),))
    return {"inputs": inputs, "col_list": col_list, "row_list": row_list, "gain_attn": gain_attn, "w_qkv": w_qkv, "w_out": w_out, "gain_ffn": gain_ffn, "w_gate": w_gate, "w_up": w_up, "w_down": w_down}


eps = 1e-06
masked = -1e+30
exact = lax.Precision.HIGHEST

def rms_scale(values, gain):
    values = values.astype(jnp.float32)
    mean_sq = lax.optimization_barrier(jnp.mean(values * values, axis=-1, keepdims=True))
    return values * lax.rsqrt(mean_sq + eps) * gain.astype(jnp.float32)

def attend(query, keys, values, allowed, scale):
    scores = jnp.einsum('lhd,khd->hlk', query.astype(jnp.float32), keys.astype(jnp.float32), precision=exact) * scale
    scores = jnp.where(allowed[None], scores, masked)
    top = lax.optimization_barrier(jnp.max(scores, axis=-1, keepdims=True))
    weights = jnp.exp(scores - top)
    probs = (weights / lax.optimization_barrier(jnp.sum(weights, axis=-1, keepdims=True))).astype(jnp.bfloat16)
    mixed = jnp.einsum('hlk,khd->lhd', probs.astype(jnp.float32), values.astype(jnp.float32), precision=exact)
    return mixed.astype(jnp.bfloat16)

def reference(inputs, col_list, row_list, gain_attn, w_qkv, w_out, gain_ffn, w_gate, w_up, w_down):
    head_dim = D // HEADS
    half = HEADS // 2
    split = half * head_dim
    scale = head_dim ** (-0.5)
    normed = rms_scale(inputs, gain_attn).astype(jnp.bfloat16)
    qkv = jnp.dot(normed.reshape(LMAX * LMAX, D), w_qkv, preferred_element_type=jnp.float32)
    qkv = qkv.astype(jnp.bfloat16).reshape(LMAX, LMAX, 3 * D)

    def heads_of(start):
        return qkv[:, :, start:start + split].reshape(LMAX, LMAX, half, head_dim)
    q_ell, k_ell, v_ell = (heads_of(0), heads_of(D), heads_of(2 * D))
    q_m, k_m, v_m = (heads_of(split), heads_of(D + split), heads_of(2 * D + split))
    here = jnp.arange(LMAX, dtype=jnp.int32)
    offset = here[None, :] - here[:, None]
    band = (offset >= -(WIN // 2)) & (offset < WIN // 2)

    def column(args):
        query, keys, values, start = args
        allowed = band & (here[None, :] >= start)
        return attend(query, keys, values, allowed, scale)
    a_ell = lax.map(column, (jnp.swapaxes(q_ell, 0, 1), jnp.swapaxes(k_ell, 0, 1), jnp.swapaxes(v_ell, 0, 1), col_list.astype(jnp.int32)))
    a_ell = jnp.swapaxes(a_ell, 0, 1)
    diff = col_list[None, :] - col_list[:, None]
    mband = (diff >= -(WIN // 2)) & (diff < WIN // 2)

    def row(args):
        query, keys, values, level = args
        allowed = mband & (col_list[None, :] <= level)
        return attend(query, keys, values, allowed, scale)
    a_m = lax.map(row, (q_m, k_m, v_m, here))
    attn = jnp.concatenate([a_ell.reshape(LMAX, LMAX, split), a_m.reshape(LMAX, LMAX, split)], axis=-1)
    resid = inputs.astype(jnp.float32) + jnp.dot(attn.reshape(LMAX * LMAX, D), w_out, preferred_element_type=jnp.float32).reshape(LMAX, LMAX, D)
    normed_ffn = rms_scale(resid, gain_ffn).astype(jnp.bfloat16).reshape(LMAX * LMAX, D)
    gate = jnp.dot(normed_ffn, w_gate, preferred_element_type=jnp.float32)
    up = jnp.dot(normed_ffn, w_up, preferred_element_type=jnp.float32)
    hidden = (jax.nn.silu(gate) * up).astype(jnp.bfloat16)
    final = resid + jnp.dot(hidden, w_down, preferred_element_type=jnp.float32).reshape(LMAX, LMAX, D)
    final = jnp.take(final, row_list.astype(jnp.int32), axis=0)
    valid = col_list[None, :] <= row_list[:, None]
    return jnp.where(valid[:, :, None], final, 0.0).astype(jnp.bfloat16)
```

```python
import functools

import jax
import jax.numpy as jnp
from jax import lax
from jax.experimental import pallas as pl
from jax.experimental.pallas import tpu as pltpu
from jax.sharding import PartitionSpec as P

HEADS = 8
WIN = 256
MESH = pl.DeviceIdType.MESH

eps = 1e-06
masked = -1e30


def rms_scale(values, gain):
    values = values.astype(jnp.float32)
    mean_sq = jnp.mean(values * values, axis=-1, keepdims=True)
    return values * lax.rsqrt(mean_sq + eps) * gain


def dot(a, b):
    return jnp.dot(a, b, preferred_element_type=jnp.float32)


def one_hot_rows(index, size):
    lanes = lax.broadcasted_iota(jnp.int32, (index.shape[0], size), 1)
    return jnp.where(lanes == index, 1.0, 0.0).astype(jnp.bfloat16)


def attention(query, key_ref, value_ref, start, width, allowed, scale, pair):
    low = lax.broadcasted_iota(jnp.int32, query.shape, 1) < pair // 2
    keys = key_ref[:, start : start + width]
    values = value_ref[:, start : start + width]
    zero = jnp.zeros_like(query)
    mixed = []
    for part in (jnp.where(low, query, zero), jnp.where(low, zero, query)):
        scores = lax.dot_general(part, keys, (((1,), (1,)), ((), ())), preferred_element_type=jnp.float32)
        scores = jnp.where(allowed, scores * scale, masked)
        top = jnp.max(scores, axis=-1, keepdims=True)
        weights = jnp.exp(scores - top)
        probs = (weights / jnp.sum(weights, axis=-1, keepdims=True)).astype(jnp.bfloat16)
        mixed.append(dot(probs, values))
    return jnp.where(low, mixed[0], mixed[1]).astype(jnp.bfloat16)


def kernel(
    n, x_ref, mc_ref, mr_ref, gain_a_ref, w_qkv_ref, w_out_ref, gain_f_ref, gate_ref, up_ref, down_ref,
    out_ref, sent, ell_out, q_buf, k_buf, v_buf, got, got_ell, attn_m, gu, dn,
    sx_send, sx_recv, sa_send, sa_recv, z_send, z_recv, x_send, x_recv, c_send, c_recv,
):
    me = lax.axis_index("harm")
    outer = n // 4
    zc, inner = me // 4, me % 4
    side, core = inner // 2, inner % 2
    other_side = zc * 4 + (1 - side) * 2 + core
    other_core = zc * 4 + side * 2 + (1 - core)
    depth = gate_ref.shape[0]
    deep = down_ref.shape[0]
    tokens, width = x_ref.shape
    block = tokens // n
    split = width // 2
    head_dim = width // HEADS
    pair = 2 * head_dim
    scale = head_dim ** (-0.5)
    step = min(tokens, 256)

    barrier = pltpu.get_barrier_semaphore()
    for d in range(1, n):
        pl.semaphore_signal(barrier, inc=1, device_id={"harm": (me + d) % n}, device_id_type=MESH)

    gu[0, pl.ds(pl.multiple_of(me * depth, depth), depth), :] = gate_ref[...]
    gu[1, pl.ds(pl.multiple_of(me * depth, depth), depth), :] = up_ref[...]
    dn[pl.ds(pl.multiple_of(me * deep, deep), deep), :] = down_ref[...]
    sent[...] = dot(one_hot_rows(mc_ref[:, 0:1], tokens), x_ref[...]).astype(jnp.bfloat16)

    pl.semaphore_wait(barrier, n - 1)

    def rows_of(ref, i):
        return ref.at[pl.ds(pl.multiple_of(i * block, block), block), :]

    def to_row(src, dst, send, recv, d):
        peer = (me + d) % n
        return pltpu.make_async_remote_copy(
            src_ref=rows_of(src, peer), dst_ref=rows_of(dst, me), send_sem=send.at[d], recv_sem=recv.at[d],
            device_id={"harm": peer}, device_id_type=MESH,
        )

    def shard(i, send, recv, slot, device):
        first = gu.at[:, pl.ds(pl.multiple_of(i * depth, depth), depth), :]
        second = dn.at[pl.ds(pl.multiple_of(i * deep, deep), deep), :]
        return [
            pltpu.make_async_remote_copy(
                src_ref=ref, dst_ref=ref, send_sem=send.at[slot, k], recv_sem=recv.at[slot, k],
                device_id={"harm": device}, device_id_type=MESH,
            )
            for k, ref in enumerate((first, second))
        ]

    def place(d, s, c):
        return ((zc + outer - d) % outer) * 4 + s * 2 + c

    pending = []

    def start(copies):
        for copy in copies:
            copy.start()
        pending.extend(copies)

    start([to_row(sent, got, sx_send, sx_recv, d) for d in range(1, n)])
    for d in range(1, outer):
        start(shard(me, z_send, z_recv, d, ((zc + d) % outer) * 4 + inner))
    start(shard(me, x_send, x_recv, 0, other_side))
    start(shard(me, c_send, c_recv, 0, other_core))
    rows_of(got, me)[...] = rows_of(sent, me)[...]

    def project(source, first):
        normed = rms_scale(source[...], gain_a_ref[...]).astype(jnp.bfloat16)
        for buf, base in ((q_buf, 0), (k_buf, width), (v_buf, 2 * width)):
            buf[...] = dot(normed, w_qkv_ref[:, base + first : base + first + split]).astype(jnp.bfloat16)

    def attend(dest, marks, level, along_ell):
        def body(i, carry):
            rows = pl.ds(pl.multiple_of(i * step, step), step)
            ell_q, col_q = mc_ref[rows, level : level + 1], mc_ref[rows, marks : marks + 1]
            ell_k, col_k = mr_ref[level : level + 1, :], mr_ref[marks : marks + 1, :]
            if along_ell:
                same, diff = col_q == col_k, ell_k - ell_q
            else:
                same, diff = ell_q == ell_k, col_k - col_q
            allowed = same & (diff >= -(WIN // 2)) & (diff < WIN // 2) & (ell_k >= col_k)
            for p in range(split // pair):
                query = q_buf[rows, p * pair : (p + 1) * pair]
                dest[rows, p * pair : (p + 1) * pair] = attention(
                    query, k_buf, v_buf, p * pair, pair, allowed, scale, pair
                )
            return carry

        lax.fori_loop(0, tokens // step, body, 0)

    project(sent, 0)
    attend(ell_out, 2, 1, True)
    start([to_row(ell_out, got_ell, sa_send, sa_recv, d) for d in range(1, n)])
    rows_of(got_ell, me)[...] = rows_of(ell_out, me)[...]

    for d in range(1, outer):
        i = place(d, side, core)
        for copy in shard(i, z_send, z_recv, d, me):
            copy.wait_recv()
        start(shard(i, x_send, x_recv, d, other_side))
        start(shard(i, c_send, c_recv, d, other_core))

    for d in range(1, n):
        to_row(sent, got, sx_send, sx_recv, d).wait_recv()
    project(got, split)
    attend(attn_m, 4, 3, False)

    for d in range(outer):
        i = place(d, 1 - side, core)
        for copy in shard(i, x_send, x_recv, d, me):
            copy.wait_recv()
        start(shard(i, c_send, c_recv, outer + d, other_core))

    for d in range(1, n):
        to_row(ell_out, got_ell, sa_send, sa_recv, d).wait_recv()
    resid = got[...].astype(jnp.float32) + (
        dot(got_ell[...], w_out_ref[:split, :]) + dot(attn_m[...], w_out_ref[split:, :])
    )
    normed_ffn = rms_scale(resid, gain_f_ref[...]).astype(jnp.bfloat16)

    for slot in range(2 * outer):
        i = place(slot % outer, side if slot < outer else 1 - side, 1 - core)
        for copy in shard(i, c_send, c_recv, slot, me):
            copy.wait_recv()
    gate = dot(normed_ffn, gu[0])
    up = dot(normed_ffn, gu[1])
    hidden = (gate / (1.0 + jnp.exp(-gate)) * up).astype(jnp.bfloat16)
    final = resid + dot(hidden, dn[...])
    valid = mc_ref[:, 4:5] <= mc_ref[:, 3:4]
    final = jnp.where(valid, final, 0.0).astype(jnp.bfloat16)
    out_ref[...] = dot(one_hot_rows(mc_ref[:, 5:6], tokens), final).astype(jnp.bfloat16)
    for copy in pending:
        copy.wait_send()


def per_device(n, inputs, col_list, row_list, gain_attn, w_qkv, w_out, gain_ffn, w_gate, w_up, w_down):
    place = lax.axis_index("harm")
    length, cols, width = inputs.shape
    rows_here = length // n
    tokens = length * cols
    split = width // 2
    my_cols = lax.dynamic_slice_in_dim(col_list, place * cols, cols)
    my_rows = lax.dynamic_slice_in_dim(row_list, place * rows_here, rows_here)
    before, after = (length, cols), (n, rows_here, cols)
    slot = jnp.arange(cols, dtype=jnp.int32)
    order = jnp.arange(tokens, dtype=jnp.int32).reshape(n, rows_here, cols).transpose(0, 1, 2)
    back = order.transpose(1, 0, 2)
    table = [
        jnp.broadcast_to(row_list[:, None] * cols + slot[None, :], before),
        jnp.broadcast_to(row_list[:, None], before),
        jnp.broadcast_to(my_cols[None, :], before),
        jnp.broadcast_to(my_rows[None, :, None], after),
        jnp.broadcast_to(col_list.reshape(n, 1, cols), after),
        back,
        back,
        back,
    ]
    by_row = jnp.stack([entry.reshape(tokens) for entry in table], axis=0)
    by_col = by_row.T
    bf16, f32 = jnp.bfloat16, jnp.float32
    depth, ff = w_gate.shape
    deep = w_down.shape[0]
    outer = n // 4
    vmem = pl.BlockSpec(memory_space=pltpu.VMEM)
    dma = pltpu.SemaphoreType.DMA
    result = pl.pallas_call(
        functools.partial(kernel, n),
        out_shape=jax.ShapeDtypeStruct((tokens, width), bf16),
        in_specs=[vmem] * 10,
        out_specs=vmem,
        scratch_shapes=[
            pltpu.VMEM((tokens, width), bf16),
            pltpu.VMEM((tokens, split), bf16),
            pltpu.VMEM((tokens, split), bf16),
            pltpu.VMEM((tokens, split), bf16),
            pltpu.VMEM((tokens, split), bf16),
            pltpu.VMEM((tokens, width), bf16),
            pltpu.VMEM((tokens, split), bf16),
            pltpu.VMEM((tokens, split), bf16),
            pltpu.VMEM((2, depth * n, ff), bf16),
            pltpu.VMEM((deep * n, width), bf16),
            dma((n,)), dma((n,)), dma((n,)), dma((n,)),
            dma((outer, 2)), dma((outer, 2)),
            dma((outer, 2)), dma((outer, 2)),
            dma((2 * outer, 2)), dma((2 * outer, 2)),
        ],
        compiler_params=pltpu.CompilerParams(
            collective_id=0, has_side_effects=True, vmem_limit_bytes=56 * 1024 * 1024
        ),
    )(
        inputs.reshape(tokens, width), by_col, by_row, gain_attn.reshape(1, width), w_qkv, w_out,
        gain_ffn.reshape(1, width), w_gate, w_up, w_down,
    )
    return result.reshape(rows_here, length, width)


def solution(mesh):
    placed = (
        P("sample", "harm", None),
        P("sample"),
        P("sample"),
        P(),
        P(),
        P(),
        P(),
        P("harm", None),
        P("harm", None),
        P("harm", None),
    )
    return jax.shard_map(
        functools.partial(per_device, mesh.shape["harm"]),
        mesh=mesh, in_specs=placed, out_specs=P("harm", "sample", None), check_vma=False,
    )
```

```python
import functools

import jax
import jax.numpy as jnp
from jax import lax
from jax.experimental import pallas as pl
from jax.experimental.pallas import tpu as pltpu
from jax.sharding import PartitionSpec as P

HEADS = 8
WIN = 256
MESH = pl.DeviceIdType.MESH

eps = 1e-06
masked = -1e30


def rms_scale(values, gain):
    values = values.astype(jnp.float32)
    mean_sq = jnp.mean(values * values, axis=-1, keepdims=True)
    return values * lax.rsqrt(mean_sq + eps) * gain


def dot(a, b):
    return jnp.dot(a, b, preferred_element_type=jnp.float32)


def one_hot_rows(index, size):
    lanes = lax.broadcasted_iota(jnp.int32, (index.shape[0], size), 1)
    return jnp.where(lanes == index, 1.0, 0.0).astype(jnp.bfloat16)


def attention(query, key_ref, value_ref, start, width, allowed, scale, pair):
    low = lax.broadcasted_iota(jnp.int32, query.shape, 1) < pair // 2
    keys = key_ref[:, start : start + width]
    values = value_ref[:, start : start + width]
    zero = jnp.zeros_like(query)
    mixed = []
    for part in (jnp.where(low, query, zero), jnp.where(low, zero, query)):
        scores = lax.dot_general(part, keys, (((1,), (1,)), ((), ())), preferred_element_type=jnp.float32)
        scores = jnp.where(allowed, scores * scale, masked)
        top = jnp.max(scores, axis=-1, keepdims=True)
        weights = jnp.exp(scores - top)
        probs = (weights / jnp.sum(weights, axis=-1, keepdims=True)).astype(jnp.bfloat16)
        mixed.append(dot(probs, values))
    return jnp.where(low, mixed[0], mixed[1]).astype(jnp.bfloat16)


def kernel(
    n, x_ref, col_ref, row_ref, gain_a_ref, w_qkv_ref, w_out_ref, gain_f_ref, gate_ref, up_ref, down_ref,
    out_ref, mc_ref, mr_ref, sent, ell_out, q_buf, k_buf, v_buf, got, got_ell, attn_m, gu, dn,
    sx_send, sx_recv, sa_send, sa_recv, z_send, z_recv, x_send, x_recv, y_send, y_recv, c_send, c_recv,
):
    me = lax.axis_index("harm")
    sample = lax.axis_index("sample")
    part = sample % 2
    other_plane = {"sample": sample + 1 - 2 * part, "harm": me}
    outer = n // 4
    zc, inner = me // 4, me % 4
    side, core = inner // 2, inner % 2
    other_side = {"harm": zc * 4 + (1 - side) * 2 + core}
    other_core = {"harm": zc * 4 + side * 2 + (1 - core)}
    depth = gate_ref.shape[0]
    deep = down_ref.shape[0]
    tokens, width = x_ref.shape
    block = tokens // n
    split = width // 2
    head_dim = width // HEADS
    pair = 2 * head_dim
    scale = head_dim ** (-0.5)
    step = min(tokens, 256)

    barrier = pltpu.get_barrier_semaphore()
    for d in range(1, n):
        pl.semaphore_signal(barrier, inc=1, device_id={"harm": (me + d) % n}, device_id_type=MESH)
    pl.semaphore_signal(barrier, inc=1, device_id=other_plane, device_id_type=MESH)

    length = col_ref.shape[1]
    cols, rows_here = tokens // length, length // n
    low_bits, mid_bits = cols.bit_length() - 1, rows_here.bit_length() - 1
    wide = lax.broadcasted_iota(jnp.int32, (length, length), 1)
    tall = lax.broadcasted_iota(jnp.int32, (length, length), 0)

    def upright(ref):
        return jnp.sum(jnp.where(wide == tall, ref[...].astype(jnp.float32), 0.0), axis=1, keepdims=True)

    def slots(shape, axis):
        t = lax.broadcasted_iota(jnp.int32, shape, axis)
        c = t & (cols - 1)
        source = t >> (low_bits + mid_bits)
        row = (t >> low_bits) & (rows_here - 1)
        return [t >> low_bits, me * cols + c, me * rows_here + row, source * cols + c]

    def fields(axis):
        shape = (tokens, length) if axis == 0 else (length, tokens)
        lists = (row_ref, col_ref, row_ref, col_ref)
        which = lax.broadcasted_iota(jnp.int32, shape, 1 - axis)
        out = []
        for ref, slot in zip(lists, slots(shape, axis)):
            values = ref[...].astype(jnp.float32) if axis == 0 else upright(ref)
            picked = jnp.where(which == slot, values, 0.0)
            out.append(jnp.sum(picked, axis=1 - axis, keepdims=True).astype(jnp.int32))
        return out

    for k, value in enumerate(fields(0)):
        mc_ref[:, k + 1 : k + 2] = value
    for k, value in enumerate(fields(1)):
        mr_ref[k + 1 : k + 2, :] = value
    t = lax.broadcasted_iota(jnp.int32, (tokens, 1), 0)
    mc_ref[:, 0:1] = mc_ref[:, 1:2] * cols + (t & (cols - 1))
    in_row = t & (length - 1)
    source = in_row >> low_bits
    row = t >> (length.bit_length() - 1)
    mc_ref[:, 5:6] = (source << (low_bits + mid_bits)) + (row << low_bits) + (in_row & (cols - 1))

    gu[0, pl.ds(pl.multiple_of(me * depth, depth), depth), :] = gate_ref[...]
    gu[1, pl.ds(pl.multiple_of(me * depth, depth), depth), :] = up_ref[...]
    dn[pl.ds(pl.multiple_of(me * deep, deep), deep), :] = down_ref[...]
    sent[...] = dot(one_hot_rows(mc_ref[:, 0:1], tokens), x_ref[...]).astype(jnp.bfloat16)

    pl.semaphore_wait(barrier, n)

    def rows_of(ref, i):
        return ref.at[pl.ds(pl.multiple_of(i * block, block), block), :]

    def to_row(src, dst, send, recv, d):
        peer = (me + d) % n
        return pltpu.make_async_remote_copy(
            src_ref=rows_of(src, peer), dst_ref=rows_of(dst, me), send_sem=send.at[d], recv_sem=recv.at[d],
            device_id={"harm": peer}, device_id_type=MESH,
        )

    def shard(i, half, send, recv, slot, device):
        copies = []
        for k, ref in enumerate((gu, dn)):
            size = (depth, deep)[k]
            first, rows = i * size, size
            if half is not None:
                rows = size // 2
                first = first + half * rows
            where = pl.ds(pl.multiple_of(first, rows), rows)
            piece = ref.at[:, where, :] if k == 0 else ref.at[where, :]
            copies.append(
                pltpu.make_async_remote_copy(
                    src_ref=piece, dst_ref=piece, send_sem=send.at[slot, k], recv_sem=recv.at[slot, k],
                    device_id=device, device_id_type=MESH,
                )
            )
        return copies

    def place(d, s, c):
        return ((zc + outer - d) % outer) * 4 + s * 2 + c

    pending = []

    def start(copies):
        for copy in copies:
            copy.start()
        pending.extend(copies)

    def arrived(copies):
        for copy in copies:
            copy.wait_recv()

    start([to_row(sent, got, sx_send, sx_recv, d) for d in range(1, n)])
    for d in range(1, outer):
        start(shard(me, part, z_send, z_recv, d, {"harm": ((zc + d) % outer) * 4 + inner}))
    start(shard(me, part, x_send, x_recv, 0, other_side))
    start(shard(me, None, c_send, c_recv, 0, other_core))
    rows_of(got, me)[...] = rows_of(sent, me)[...]

    def project(source, first):
        normed = rms_scale(source[...], gain_a_ref[...]).astype(jnp.bfloat16)
        for buf, base in ((q_buf, 0), (k_buf, width), (v_buf, 2 * width)):
            buf[...] = dot(normed, w_qkv_ref[:, base + first : base + first + split]).astype(jnp.bfloat16)

    def attend(dest, marks, level, along_ell):
        def body(i, carry):
            rows = pl.ds(pl.multiple_of(i * step, step), step)
            ell_q, col_q = mc_ref[rows, level : level + 1], mc_ref[rows, marks : marks + 1]
            ell_k, col_k = mr_ref[level : level + 1, :], mr_ref[marks : marks + 1, :]
            if along_ell:
                same, diff = col_q == col_k, ell_k - ell_q
            else:
                same, diff = ell_q == ell_k, col_k - col_q
            allowed = same & (diff >= -(WIN // 2)) & (diff < WIN // 2) & (ell_k >= col_k)
            for p in range(split // pair):
                query = q_buf[rows, p * pair : (p + 1) * pair]
                dest[rows, p * pair : (p + 1) * pair] = attention(
                    query, k_buf, v_buf, p * pair, pair, allowed, scale, pair
                )
            return carry

        lax.fori_loop(0, tokens // step, body, 0)

    project(sent, 0)
    attend(ell_out, 2, 1, True)
    start([to_row(ell_out, got_ell, sa_send, sa_recv, d) for d in range(1, n)])
    rows_of(got_ell, me)[...] = rows_of(ell_out, me)[...]

    for d in range(1, outer):
        i = place(d, side, core)
        arrived(shard(i, part, z_send, z_recv, d, other_core))
        start(shard(i, part, x_send, x_recv, d, other_side))
        start(shard(i, part, y_send, y_recv, d, other_plane))
        start(shard(i, part, c_send, c_recv, d, other_core))

    for d in range(1, n):
        to_row(sent, got, sx_send, sx_recv, d).wait_recv()
    project(got, split)
    attend(attn_m, 4, 3, False)

    for d in range(outer):
        i = place(d, 1 - side, core)
        arrived(shard(i, part, x_send, x_recv, d, other_side))
        start(shard(i, part, y_send, y_recv, outer + d, other_plane))
        start(shard(i, part, c_send, c_recv, outer + d, other_core))

    for slot in range(1, 2 * outer):
        i = place(slot % outer, side if slot < outer else 1 - side, core)
        arrived(shard(i, 1 - part, y_send, y_recv, slot, other_plane))
        start(shard(i, 1 - part, c_send, c_recv, 2 * outer + slot, other_core))

    for d in range(1, n):
        to_row(ell_out, got_ell, sa_send, sa_recv, d).wait_recv()
    resid = got[...].astype(jnp.float32) + (
        dot(got_ell[...], w_out_ref[:split, :]) + dot(attn_m[...], w_out_ref[split:, :])
    )
    normed_ffn = rms_scale(resid, gain_f_ref[...]).astype(jnp.bfloat16)

    arrived(shard(place(0, side, 1 - core), None, c_send, c_recv, 0, other_core))
    for slot in range(1, 2 * outer):
        i = place(slot % outer, side if slot < outer else 1 - side, 1 - core)
        arrived(shard(i, part, c_send, c_recv, slot, other_core))
        arrived(shard(i, 1 - part, c_send, c_recv, 2 * outer + slot, other_core))
    gate = dot(normed_ffn, gu[0])
    up = dot(normed_ffn, gu[1])
    hidden = (gate / (1.0 + jnp.exp(-gate)) * up).astype(jnp.bfloat16)
    final = resid + dot(hidden, dn[...])
    valid = mc_ref[:, 4:5] <= mc_ref[:, 3:4]
    final = jnp.where(valid, final, 0.0).astype(jnp.bfloat16)
    out_ref[...] = dot(one_hot_rows(mc_ref[:, 5:6], tokens), final).astype(jnp.bfloat16)
    for copy in pending:
        copy.wait_send()


def per_device(n, inputs, col_list, row_list, gain_attn, w_qkv, w_out, gain_ffn, w_gate, w_up, w_down):
    length, cols, width = inputs.shape
    rows_here = length // n
    tokens = length * cols
    split = width // 2
    bf16 = jnp.bfloat16
    depth, ff = w_gate.shape
    deep = w_down.shape[0]
    outer = n // 4
    vmem = pl.BlockSpec(memory_space=pltpu.VMEM)
    dma = pltpu.SemaphoreType.DMA
    result = pl.pallas_call(
        functools.partial(kernel, n),
        out_shape=jax.ShapeDtypeStruct((tokens, width), bf16),
        in_specs=[vmem] * 10,
        out_specs=vmem,
        scratch_shapes=[
            pltpu.VMEM((tokens, 8), jnp.int32),
            pltpu.VMEM((8, tokens), jnp.int32),
            pltpu.VMEM((tokens, width), bf16),
            pltpu.VMEM((tokens, split), bf16),
            pltpu.VMEM((tokens, split), bf16),
            pltpu.VMEM((tokens, split), bf16),
            pltpu.VMEM((tokens, split), bf16),
            pltpu.VMEM((tokens, width), bf16),
            pltpu.VMEM((tokens, split), bf16),
            pltpu.VMEM((tokens, split), bf16),
            pltpu.VMEM((2, depth * n, ff), bf16),
            pltpu.VMEM((deep * n, width), bf16),
            dma((n,)), dma((n,)), dma((n,)), dma((n,)),
            dma((outer, 2)), dma((outer, 2)),
            dma((outer, 2)), dma((outer, 2)),
            dma((2 * outer, 2)), dma((2 * outer, 2)),
            dma((4 * outer, 2)), dma((4 * outer, 2)),
        ],
        compiler_params=pltpu.CompilerParams(
            collective_id=0, has_side_effects=True, vmem_limit_bytes=56 * 1024 * 1024
        ),
    )(
        inputs.reshape(tokens, width), col_list.reshape(1, length), row_list.reshape(1, length), gain_attn.reshape(1, width), w_qkv, w_out,
        gain_ffn.reshape(1, width), w_gate, w_up, w_down,
    )
    return result.reshape(rows_here, length, width)


def solution(mesh):
    placed = (
        P("sample", "harm", None),
        P("sample"),
        P("sample"),
        P(),
        P(),
        P(),
        P(),
        P("harm", None),
        P("harm", None),
        P("harm", None),
    )
    return jax.shard_map(
        functools.partial(per_device, mesh.shape["harm"]),
        mesh=mesh, in_specs=placed, out_specs=P("harm", "sample", None), check_vma=False,
    )
```

```python
import functools

import jax
import jax.numpy as jnp
from jax import lax
from jax.experimental import pallas as pl
from jax.experimental.pallas import tpu as pltpu
from jax.sharding import PartitionSpec as P

HEADS = 8
WIN = 256
MESH = pl.DeviceIdType.MESH

eps = 1e-06
masked = -1e30


def rms_scale(values, gain):
    values = values.astype(jnp.float32)
    mean_sq = jnp.mean(values * values, axis=-1, keepdims=True)
    return values * lax.rsqrt(mean_sq + eps) * gain


def dot(a, b):
    return jnp.dot(a, b, preferred_element_type=jnp.float32)


def one_hot_rows(index, size):
    lanes = lax.broadcasted_iota(jnp.int32, (index.shape[0], size), 1)
    return jnp.where(lanes == index, 1.0, 0.0).astype(jnp.bfloat16)


def attention(query, key_ref, value_ref, start, width, allowed, scale, pair):
    low = lax.broadcasted_iota(jnp.int32, query.shape, 1) < pair // 2
    keys = key_ref[:, start : start + width]
    values = value_ref[:, start : start + width]
    zero = jnp.zeros_like(query)
    mixed = []
    for part in (jnp.where(low, query, zero), jnp.where(low, zero, query)):
        scores = lax.dot_general(part, keys, (((1,), (1,)), ((), ())), preferred_element_type=jnp.float32)
        scores = jnp.where(allowed, scores * scale, masked)
        top = jnp.max(scores, axis=-1, keepdims=True)
        weights = jnp.exp(scores - top)
        probs = (weights / jnp.sum(weights, axis=-1, keepdims=True)).astype(jnp.bfloat16)
        mixed.append(dot(probs, values))
    return jnp.where(low, mixed[0], mixed[1]).astype(jnp.bfloat16)


def kernel(
    n, x_ref, col_ref, row_ref, gain_a_ref, w_qkv_ref, w_out_ref, gain_f_ref, gate_ref, up_ref, down_ref,
    out_ref, mc_ref, mr_ref, sent, ell_out, q_buf, k_buf, v_buf, got, got_ell, attn_m, gu, dn,
    sx_send, sx_recv, sa_send, sa_recv, z_send, z_recv, x_send, x_recv, y_send, y_recv, c_send, c_recv,
):
    me = lax.axis_index("harm")
    sample = lax.axis_index("sample")
    part = sample % 2
    other_plane = {"sample": sample + 1 - 2 * part, "harm": me}
    outer = n // 4
    zc, inner = me // 4, me % 4
    side, core = inner // 2, inner % 2
    other_side = {"harm": zc * 4 + (1 - side) * 2 + core}
    other_core = {"harm": zc * 4 + side * 2 + (1 - core)}
    depth = gate_ref.shape[0]
    deep = down_ref.shape[0]
    tokens, width = x_ref.shape
    block = tokens // n
    split = width // 2
    head_dim = width // HEADS
    pair = 2 * head_dim
    scale = head_dim ** (-0.5)
    step = min(tokens, 256)

    barrier = pltpu.get_barrier_semaphore()
    for d in range(1, n):
        pl.semaphore_signal(barrier, inc=1, device_id={"harm": (me + d) % n}, device_id_type=MESH)
    pl.semaphore_signal(barrier, inc=1, device_id=other_plane, device_id_type=MESH)

    length = col_ref.shape[1]
    cols, rows_here = tokens // length, length // n
    low_bits, mid_bits = cols.bit_length() - 1, rows_here.bit_length() - 1
    wide = lax.broadcasted_iota(jnp.int32, (length, length), 1)
    tall = lax.broadcasted_iota(jnp.int32, (length, length), 0)

    def upright(ref):
        return jnp.sum(jnp.where(wide == tall, ref[...].astype(jnp.float32), 0.0), axis=1, keepdims=True)

    def slots(shape, axis):
        t = lax.broadcasted_iota(jnp.int32, shape, axis)
        c = t & (cols - 1)
        source = t >> (low_bits + mid_bits)
        row = (t >> low_bits) & (rows_here - 1)
        return [t >> low_bits, me * cols + c, me * rows_here + row, source * cols + c]

    def fields(axis):
        shape = (tokens, length) if axis == 0 else (length, tokens)
        lists = (row_ref, col_ref, row_ref, col_ref)
        which = lax.broadcasted_iota(jnp.int32, shape, 1 - axis)
        out = []
        for ref, slot in zip(lists, slots(shape, axis)):
            values = ref[...].astype(jnp.float32) if axis == 0 else upright(ref)
            picked = jnp.where(which == slot, values, 0.0)
            out.append(jnp.sum(picked, axis=1 - axis, keepdims=True).astype(jnp.int32))
        return out

    for k, value in enumerate(fields(0)):
        mc_ref[:, k + 1 : k + 2] = value
    for k, value in enumerate(fields(1)):
        mr_ref[k + 1 : k + 2, :] = value
    t = lax.broadcasted_iota(jnp.int32, (tokens, 1), 0)
    mc_ref[:, 0:1] = mc_ref[:, 1:2] * cols + (t & (cols - 1))
    in_row = t & (length - 1)
    source = in_row >> low_bits
    row = t >> (length.bit_length() - 1)
    mc_ref[:, 5:6] = (source << (low_bits + mid_bits)) + (row << low_bits) + (in_row & (cols - 1))

    gu[0, pl.ds(pl.multiple_of(me * depth, depth), depth), :] = gate_ref[...]
    gu[1, pl.ds(pl.multiple_of(me * depth, depth), depth), :] = up_ref[...]
    dn[pl.ds(pl.multiple_of(me * deep, deep), deep), :] = down_ref[...]
    sent[...] = dot(one_hot_rows(mc_ref[:, 0:1], tokens), x_ref[...]).astype(jnp.bfloat16)

    pl.semaphore_wait(barrier, n)

    def rows_of(ref, i):
        return ref.at[pl.ds(pl.multiple_of(i * block, block), block), :]

    def to_row(src, dst, send, recv, d):
        peer = (me + d) % n
        return pltpu.make_async_remote_copy(
            src_ref=rows_of(src, peer), dst_ref=rows_of(dst, me), send_sem=send.at[d], recv_sem=recv.at[d],
            device_id={"harm": peer}, device_id_type=MESH,
        )

    def pieces(i, halves, send, recv, slot, device):
        copies = []
        for k, ref in enumerate((gu, dn)):
            half = halves[k]
            if half is None:
                continue
            size = (depth, deep)[k]
            first, rows = i * size, size
            if half is not whole:
                rows = size // 2
                first = first + half * rows
            where = pl.ds(pl.multiple_of(first, rows), rows)
            piece = ref.at[:, where, :] if k == 0 else ref.at[where, :]
            copies.append(
                pltpu.make_async_remote_copy(
                    src_ref=piece, dst_ref=piece, send_sem=send.at[slot, k], recv_sem=recv.at[slot, k],
                    device_id=device, device_id_type=MESH,
                )
            )
        return copies

    whole = "all"
    full, mine, theirs = (whole, whole), (part, whole), (1 - part, None)
    traded = (part, None)

    def place(z, s, c):
        return z * 4 + s * 2 + c

    pending = []

    def guard(cond, body):
        if cond is None:
            body()
        else:
            pl.when(cond)(body)

    def start(build, cond=None):
        def body():
            for copy in build():
                copy.start()

        guard(cond, body)
        pending.append((cond, build))

    def arrived(build, cond=None):
        def body():
            for copy in build():
                copy.wait_recv()

        guard(cond, body)

    def send(cond, *args):
        start(lambda: pieces(*args), cond)

    def receive(cond, *args):
        arrived(lambda: pieces(*args), cond)

    def both(a, b):
        return b if a is None else a & b

    def reached(t):
        if t == 0:
            return [(zc, None, 0)]
        return [(zc - t, zc - t >= 0, 0), (zc + t, zc + t < outer, 1)]

    def along_z(t, z, cond, stream):
        step_z = 1 - 2 * stream
        ahead = zc + step_z
        ok = both(cond, (ahead < outer) if stream == 0 else (ahead >= 0))
        if t + 1 < outer:
            device = {"harm": ahead * 4 + inner}
            send(ok, place(z, side, core), mine, z_send, z_recv, stream * outer + t + 1, device)

    def z_stage(t):
        for z, cond, stream in reached(t):
            i = place(z, side, core)
            receive(cond, i, mine, z_send, z_recv, stream * outer + t, other_core)
            along_z(t, z, cond, stream)
            send(cond, i, mine, x_send, x_recv, z, other_side)
            send(cond, i, traded, y_send, y_recv, z, other_plane)
            send(cond, i, mine, c_send, c_recv, z, other_core)

    def x_stage(t):
        for z, cond, stream in reached(t):
            i = place(z, 1 - side, core)
            receive(cond, i, mine, x_send, x_recv, z, other_side)
            send(cond, i, traded, y_send, y_recv, outer + z, other_plane)
            send(cond, i, mine, c_send, c_recv, outer + z, other_core)

    def y_stage(t, other):
        for z, cond, stream in reached(t):
            i = place(z, 1 - side if other else side, core)
            slot = outer * other + z
            receive(cond, i, theirs, y_send, y_recv, slot, other_plane)
            send(cond, i, theirs, c_send, c_recv, 2 * outer + slot, other_core)

    def core_stage(t, other):
        for z, cond, stream in reached(t):
            i = place(z, 1 - side if other else side, 1 - core)
            slot = outer * other + z
            if t == 0 and not other:
                receive(None, i, full, c_send, c_recv, slot, other_core)
            else:
                receive(cond, i, mine, c_send, c_recv, slot, other_core)
                receive(cond, i, theirs, c_send, c_recv, 2 * outer + slot, other_core)

    def tokens_out(src, dst, send_sem, recv_sem):
        return lambda: [to_row(src, dst, send_sem, recv_sem, d) for d in range(1, n)]

    for stream in (0, 1):
        along_z(0, zc, None, stream)
    send(None, me, mine, x_send, x_recv, zc, other_side)
    send(None, me, full, c_send, c_recv, zc, other_core)
    start(tokens_out(sent, got, sx_send, sx_recv))
    rows_of(got, me)[...] = rows_of(sent, me)[...]

    def project(source, first):
        normed = rms_scale(source[...], gain_a_ref[...]).astype(jnp.bfloat16)
        for buf, base in ((q_buf, 0), (k_buf, width), (v_buf, 2 * width)):
            buf[...] = dot(normed, w_qkv_ref[:, base + first : base + first + split]).astype(jnp.bfloat16)

    def attend(dest, marks, level, along_ell):
        def body(i, carry):
            rows = pl.ds(pl.multiple_of(i * step, step), step)
            ell_q, col_q = mc_ref[rows, level : level + 1], mc_ref[rows, marks : marks + 1]
            ell_k, col_k = mr_ref[level : level + 1, :], mr_ref[marks : marks + 1, :]
            if along_ell:
                same, diff = col_q == col_k, ell_k - ell_q
            else:
                same, diff = ell_q == ell_k, col_k - col_q
            allowed = same & (diff >= -(WIN // 2)) & (diff < WIN // 2) & (ell_k >= col_k)
            for p in range(split // pair):
                query = q_buf[rows, p * pair : (p + 1) * pair]
                dest[rows, p * pair : (p + 1) * pair] = attention(
                    query, k_buf, v_buf, p * pair, pair, allowed, scale, pair
                )
            return carry

        lax.fori_loop(0, tokens // step, body, 0)

    project(sent, 0)
    z_stage(1)
    attend(ell_out, 2, 1, True)
    start(tokens_out(ell_out, got_ell, sa_send, sa_recv))
    rows_of(got_ell, me)[...] = rows_of(ell_out, me)[...]

    x_stage(0)
    for t in range(2, outer):
        z_stage(t)
        x_stage(t - 1)
    y_stage(0, 1)
    arrived(tokens_out(sent, got, sx_send, sx_recv))
    project(got, split)
    x_stage(outer - 1)
    attend(attn_m, 4, 3, False)
    for t in range(1, outer):
        y_stage(t, 0)
        y_stage(t, 1)

    arrived(tokens_out(ell_out, got_ell, sa_send, sa_recv))
    resid = got[...].astype(jnp.float32) + (
        dot(got_ell[...], w_out_ref[:split, :]) + dot(attn_m[...], w_out_ref[split:, :])
    )
    normed_ffn = rms_scale(resid, gain_f_ref[...]).astype(jnp.bfloat16)

    for t in range(outer):
        for other in (0, 1):
            core_stage(t, other)
    gate = dot(normed_ffn, gu[0])
    up = dot(normed_ffn, gu[1])
    hidden = (gate / (1.0 + jnp.exp(-gate)) * up).astype(jnp.bfloat16)
    final = resid + dot(hidden, dn[...])
    valid = mc_ref[:, 4:5] <= mc_ref[:, 3:4]
    final = jnp.where(valid, final, 0.0).astype(jnp.bfloat16)
    out_ref[...] = dot(one_hot_rows(mc_ref[:, 5:6], tokens), final).astype(jnp.bfloat16)
    for cond, build in pending:

        def finish(build=build):
            for copy in build():
                copy.wait_send()

        guard(cond, finish)


def per_device(n, inputs, col_list, row_list, gain_attn, w_qkv, w_out, gain_ffn, w_gate, w_up, w_down):
    length, cols, width = inputs.shape
    rows_here = length // n
    tokens = length * cols
    split = width // 2
    bf16 = jnp.bfloat16
    depth, ff = w_gate.shape
    deep = w_down.shape[0]
    outer = n // 4
    vmem = pl.BlockSpec(memory_space=pltpu.VMEM)
    dma = pltpu.SemaphoreType.DMA
    result = pl.pallas_call(
        functools.partial(kernel, n),
        out_shape=jax.ShapeDtypeStruct((tokens, width), bf16),
        in_specs=[vmem] * 10,
        out_specs=vmem,
        scratch_shapes=[
            pltpu.VMEM((tokens, 8), jnp.int32),
            pltpu.VMEM((8, tokens), jnp.int32),
            pltpu.VMEM((tokens, width), bf16),
            pltpu.VMEM((tokens, split), bf16),
            pltpu.VMEM((tokens, split), bf16),
            pltpu.VMEM((tokens, split), bf16),
            pltpu.VMEM((tokens, split), bf16),
            pltpu.VMEM((tokens, width), bf16),
            pltpu.VMEM((tokens, split), bf16),
            pltpu.VMEM((tokens, split), bf16),
            pltpu.VMEM((2, depth * n, ff), bf16),
            pltpu.VMEM((deep * n, width), bf16),
            dma((n,)), dma((n,)), dma((n,)), dma((n,)),
            dma((2 * outer, 2)), dma((2 * outer, 2)),
            dma((outer, 2)), dma((outer, 2)),
            dma((2 * outer, 2)), dma((2 * outer, 2)),
            dma((4 * outer, 2)), dma((4 * outer, 2)),
        ],
        compiler_params=pltpu.CompilerParams(
            collective_id=0, has_side_effects=True, vmem_limit_bytes=56 * 1024 * 1024
        ),
    )(
        inputs.reshape(tokens, width), col_list.reshape(1, length), row_list.reshape(1, length), gain_attn.reshape(1, width), w_qkv, w_out,
        gain_ffn.reshape(1, width), w_gate, w_up, w_down,
    )
    return result.reshape(rows_here, length, width)


def solution(mesh):
    placed = (
        P("sample", "harm", None),
        P("sample"),
        P("sample"),
        P(),
        P(),
        P(),
        P(),
        P("harm", None),
        P("harm", None),
        P("harm", None),
    )
    return jax.shard_map(
        functools.partial(per_device, mesh.shape["harm"]),
        mesh=mesh, in_specs=placed, out_specs=P("harm", "sample", None), check_vma=False,
    )
```

```python
import functools

import jax
import jax.numpy as jnp
from jax import lax
from jax.experimental import pallas as pl
from jax.experimental.pallas import tpu as pltpu
from jax.sharding import PartitionSpec as P

HEADS = 8
WIN = 256
MESH = pl.DeviceIdType.MESH

eps = 1e-06
masked = -1e30


def rms_scale(values, gain):
    values = values.astype(jnp.float32)
    mean_sq = jnp.mean(values * values, axis=-1, keepdims=True)
    return values * lax.rsqrt(mean_sq + eps) * gain


def dot(a, b):
    return jnp.dot(a, b, preferred_element_type=jnp.float32)


def one_hot_rows(index, size):
    lanes = lax.broadcasted_iota(jnp.int32, (index.shape[0], size), 1)
    return jnp.where(lanes == index, 1.0, 0.0).astype(jnp.bfloat16)


def attention(query, key_ref, value_ref, start, width, allowed, scale, pair):
    low = lax.broadcasted_iota(jnp.int32, query.shape, 1) < pair // 2
    keys = key_ref[:, start : start + width]
    values = value_ref[:, start : start + width]
    zero = jnp.zeros_like(query)
    mixed = []
    for part in (jnp.where(low, query, zero), jnp.where(low, zero, query)):
        scores = lax.dot_general(part, keys, (((1,), (1,)), ((), ())), preferred_element_type=jnp.float32)
        scores = jnp.where(allowed, scores * scale, masked)
        top = jnp.max(scores, axis=-1, keepdims=True)
        weights = jnp.exp(scores - top)
        probs = (weights / jnp.sum(weights, axis=-1, keepdims=True)).astype(jnp.bfloat16)
        mixed.append(dot(probs, values))
    return jnp.where(low, mixed[0], mixed[1]).astype(jnp.bfloat16)


def kernel(
    n, x_ref, col_ref, row_ref, gain_a_ref, w_qkv_hbm, w_out_hbm, gain_f_ref, gate_ref, up_ref, down_ref,
    out_ref, w_qkv_ref, w_out_ref, w_sem, mc_ref, mr_ref, sent, ell_out, q_buf, k_buf, v_buf, got, got_ell, attn_m, gu, dn,
    sx_send, sx_recv, sa_send, sa_recv, z_send, z_recv, x_send, x_recv, y_send, y_recv, c_send, c_recv,
):
    me = lax.axis_index("harm")
    sample = lax.axis_index("sample")
    part = sample % 2
    other_plane = {"sample": sample + 1 - 2 * part, "harm": me}
    outer = n // 4
    zc, inner = me // 4, me % 4
    side, core = inner // 2, inner % 2
    other_side = {"harm": zc * 4 + (1 - side) * 2 + core}
    other_core = {"harm": zc * 4 + side * 2 + (1 - core)}
    depth = gate_ref.shape[0]
    deep = down_ref.shape[0]
    tokens, width = x_ref.shape[0] * x_ref.shape[1], x_ref.shape[2]
    block = tokens // n
    split = width // 2
    head_dim = width // HEADS
    pair = 2 * head_dim
    scale = head_dim ** (-0.5)
    step = min(tokens, 256)

    fetch_qkv = pltpu.make_async_copy(w_qkv_hbm, w_qkv_ref, w_sem.at[0])
    fetch_out = pltpu.make_async_copy(w_out_hbm, w_out_ref, w_sem.at[1])
    fetch_qkv.start()
    fetch_out.start()
    barrier = pltpu.get_barrier_semaphore()
    for d in range(1, n):
        pl.semaphore_signal(barrier, inc=1, device_id={"harm": (me + d) % n}, device_id_type=MESH)
    pl.semaphore_signal(barrier, inc=1, device_id=other_plane, device_id_type=MESH)

    length = col_ref.shape[1]
    cols, rows_here = tokens // length, length // n
    low_bits, mid_bits = cols.bit_length() - 1, rows_here.bit_length() - 1
    wide = lax.broadcasted_iota(jnp.int32, (length, length), 1)
    tall = lax.broadcasted_iota(jnp.int32, (length, length), 0)

    def upright(ref):
        return jnp.sum(jnp.where(wide == tall, ref[...].astype(jnp.float32), 0.0), axis=1, keepdims=True)

    def slots(shape, axis):
        t = lax.broadcasted_iota(jnp.int32, shape, axis)
        c = t & (cols - 1)
        source = t >> (low_bits + mid_bits)
        row = (t >> low_bits) & (rows_here - 1)
        return [t >> low_bits, me * cols + c, me * rows_here + row, source * cols + c]

    def fields(axis):
        shape = (tokens, length) if axis == 0 else (length, tokens)
        lists = (row_ref, col_ref, row_ref, col_ref)
        which = lax.broadcasted_iota(jnp.int32, shape, 1 - axis)
        out = []
        for ref, slot in zip(lists, slots(shape, axis)):
            values = ref[...].astype(jnp.float32) if axis == 0 else upright(ref)
            picked = jnp.where(which == slot, values, 0.0)
            out.append(jnp.sum(picked, axis=1 - axis, keepdims=True).astype(jnp.int32))
        return out

    for k, value in enumerate(fields(0)):
        mc_ref[:, k + 1 : k + 2] = value
    for k, value in enumerate(fields(1)):
        mr_ref[k + 1 : k + 2, :] = value
    t = lax.broadcasted_iota(jnp.int32, (tokens, 1), 0)
    mc_ref[:, 0:1] = mc_ref[:, 1:2] * cols + (t & (cols - 1))
    in_row = t & (length - 1)
    source = in_row >> low_bits
    row = t >> (length.bit_length() - 1)
    mc_ref[:, 5:6] = (source << (low_bits + mid_bits)) + (row << low_bits) + (in_row & (cols - 1))

    gu[0, pl.ds(pl.multiple_of(me * depth, depth), depth), :] = gate_ref[...]
    gu[1, pl.ds(pl.multiple_of(me * depth, depth), depth), :] = up_ref[...]
    dn[pl.ds(pl.multiple_of(me * deep, deep), deep), :] = down_ref[...]
    sent[...] = dot(one_hot_rows(mc_ref[:, 0:1], tokens), x_ref[...].reshape(tokens, width)).astype(jnp.bfloat16)

    pl.semaphore_wait(barrier, n)

    def rows_of(ref, i):
        return ref.at[pl.ds(pl.multiple_of(i * block, block), block), :]

    def to_row(src, dst, send, recv, d):
        peer = (me + d) % n
        return pltpu.make_async_remote_copy(
            src_ref=rows_of(src, peer), dst_ref=rows_of(dst, me), send_sem=send.at[d], recv_sem=recv.at[d],
            device_id={"harm": peer}, device_id_type=MESH,
        )

    def pieces(i, halves, send, recv, slot, device):
        copies = []
        for k, ref in enumerate((gu, dn)):
            half = halves[k]
            if half is None:
                continue
            size = (depth, deep)[k]
            first, rows = i * size, size
            if half is not whole:
                rows = size // 2
                first = first + half * rows
            where = pl.ds(pl.multiple_of(first, rows), rows)
            piece = ref.at[:, where, :] if k == 0 else ref.at[where, :]
            copies.append(
                pltpu.make_async_remote_copy(
                    src_ref=piece, dst_ref=piece, send_sem=send.at[slot, k], recv_sem=recv.at[slot, k],
                    device_id=device, device_id_type=MESH,
                )
            )
        return copies

    whole = "all"
    full, mine, theirs = (whole, whole), (part, part), (1 - part, 1 - part)
    traded = (part, part)

    def place(z, s, c):
        return z * 4 + s * 2 + c

    pending = []

    def guard(cond, body):
        if cond is None:
            body()
        else:
            pl.when(cond)(body)

    def start(build, cond=None):
        def body():
            for copy in build():
                copy.start()

        guard(cond, body)
        pending.append((cond, build))

    def arrived(build, cond=None):
        def body():
            for copy in build():
                copy.wait_recv()

        guard(cond, body)

    def send(cond, *args):
        start(lambda: pieces(*args), cond)

    def receive(cond, *args):
        arrived(lambda: pieces(*args), cond)

    def both(a, b):
        return b if a is None else a & b

    def reached(t):
        if t == 0:
            return [(zc, None, 0)]
        return [(zc - t, zc - t >= 0, 0), (zc + t, zc + t < outer, 1)]

    def along_z(t, z, cond, stream):
        step_z = 1 - 2 * stream
        ahead = zc + step_z
        ok = both(cond, (ahead < outer) if stream == 0 else (ahead >= 0))
        if t + 1 < outer:
            device = {"harm": ahead * 4 + inner}
            send(ok, place(z, side, core), mine, z_send, z_recv, stream * outer + t + 1, device)

    def z_stage(t):
        for z, cond, stream in reached(t):
            i = place(z, side, core)
            receive(cond, i, mine, z_send, z_recv, stream * outer + t, other_core)
            along_z(t, z, cond, stream)
            send(cond, i, mine, x_send, x_recv, z, other_side)
            send(cond, i, traded, y_send, y_recv, z, other_plane)
            send(cond, i, mine, c_send, c_recv, z, other_core)

    def x_stage(t):
        for z, cond, stream in reached(t):
            i = place(z, 1 - side, core)
            receive(cond, i, mine, x_send, x_recv, z, other_side)
            send(cond, i, traded, y_send, y_recv, outer + z, other_plane)
            send(cond, i, mine, c_send, c_recv, outer + z, other_core)

    def y_stage(t, other):
        for z, cond, stream in reached(t):
            i = place(z, 1 - side if other else side, core)
            slot = outer * other + z
            receive(cond, i, theirs, y_send, y_recv, slot, other_plane)
            send(cond, i, theirs, c_send, c_recv, 2 * outer + slot, other_core)

    def core_stage(t, other):
        for z, cond, stream in reached(t):
            i = place(z, 1 - side if other else side, 1 - core)
            slot = outer * other + z
            if t == 0 and not other:
                receive(None, i, full, c_send, c_recv, slot, other_core)
            else:
                receive(cond, i, mine, c_send, c_recv, slot, other_core)
                receive(cond, i, theirs, c_send, c_recv, 2 * outer + slot, other_core)

    def tokens_out(src, dst, send_sem, recv_sem):
        return lambda: [to_row(src, dst, send_sem, recv_sem, d) for d in range(1, n)]

    for stream in (0, 1):
        along_z(0, zc, None, stream)
    send(None, me, mine, x_send, x_recv, zc, other_side)
    send(None, me, full, c_send, c_recv, zc, other_core)
    start(tokens_out(sent, got, sx_send, sx_recv))
    rows_of(got, me)[...] = rows_of(sent, me)[...]

    def project(source, first):
        normed = rms_scale(source[...], gain_a_ref[...]).astype(jnp.bfloat16)
        for buf, base in ((q_buf, 0), (k_buf, width), (v_buf, 2 * width)):
            buf[...] = dot(normed, w_qkv_ref[:, base + first : base + first + split]).astype(jnp.bfloat16)

    def attend(dest, marks, level, along_ell):
        def body(i, carry):
            rows = pl.ds(pl.multiple_of(i * step, step), step)
            ell_q, col_q = mc_ref[rows, level : level + 1], mc_ref[rows, marks : marks + 1]
            ell_k, col_k = mr_ref[level : level + 1, :], mr_ref[marks : marks + 1, :]
            if along_ell:
                same, diff = col_q == col_k, ell_k - ell_q
            else:
                same, diff = ell_q == ell_k, col_k - col_q
            allowed = same & (diff >= -(WIN // 2)) & (diff < WIN // 2) & (ell_k >= col_k)
            for p in range(split // pair):
                query = q_buf[rows, p * pair : (p + 1) * pair]
                dest[rows, p * pair : (p + 1) * pair] = attention(
                    query, k_buf, v_buf, p * pair, pair, allowed, scale, pair
                )
            return carry

        lax.fori_loop(0, tokens // step, body, 0)

    fetch_qkv.wait()
    project(sent, 0)
    z_stage(1)
    attend(ell_out, 2, 1, True)
    start(tokens_out(ell_out, got_ell, sa_send, sa_recv))
    rows_of(got_ell, me)[...] = rows_of(ell_out, me)[...]

    x_stage(0)
    for t in range(2, outer):
        z_stage(t)
        x_stage(t - 1)
    y_stage(0, 1)
    arrived(tokens_out(sent, got, sx_send, sx_recv))
    project(got, split)
    x_stage(outer - 1)
    attend(attn_m, 4, 3, False)
    for t in range(1, outer):
        y_stage(t, 0)
        y_stage(t, 1)

    arrived(tokens_out(ell_out, got_ell, sa_send, sa_recv))
    fetch_out.wait()
    resid = got[...].astype(jnp.float32) + (
        dot(got_ell[...], w_out_ref[:split, :]) + dot(attn_m[...], w_out_ref[split:, :])
    )
    normed_ffn = rms_scale(resid, gain_f_ref[...]).astype(jnp.bfloat16)

    for t in range(outer):
        for other in (0, 1):
            core_stage(t, other)
    gate = dot(normed_ffn, gu[0])
    up = dot(normed_ffn, gu[1])
    hidden = (gate / (1.0 + jnp.exp(-gate)) * up).astype(jnp.bfloat16)
    final = resid + dot(hidden, dn[...])
    valid = mc_ref[:, 4:5] <= mc_ref[:, 3:4]
    final = jnp.where(valid, final, 0.0).astype(jnp.bfloat16)
    out_ref[...] = dot(one_hot_rows(mc_ref[:, 5:6], tokens), final).astype(jnp.bfloat16)
    for cond, build in pending:

        def finish(build=build):
            for copy in build():
                copy.wait_send()

        guard(cond, finish)


def per_device(n, inputs, col_list, row_list, gain_attn, w_qkv, w_out, gain_ffn, w_gate, w_up, w_down):
    length, cols, width = inputs.shape
    rows_here = length // n
    tokens = length * cols
    split = width // 2
    bf16 = jnp.bfloat16
    depth, ff = w_gate.shape
    deep = w_down.shape[0]
    outer = n // 4
    vmem = pl.BlockSpec(memory_space=pltpu.VMEM)
    hbm = pl.BlockSpec(memory_space=pl.ANY)
    dma = pltpu.SemaphoreType.DMA
    result = pl.pallas_call(
        functools.partial(kernel, n),
        out_shape=jax.ShapeDtypeStruct((tokens, width), bf16),
        in_specs=[vmem] * 4 + [hbm] * 2 + [vmem] * 4,
        out_specs=vmem,
        scratch_shapes=[
            pltpu.VMEM(w_qkv.shape, bf16),
            pltpu.VMEM(w_out.shape, bf16),
            dma((2,)),
            pltpu.VMEM((tokens, 8), jnp.int32),
            pltpu.VMEM((8, tokens), jnp.int32),
            pltpu.VMEM((tokens, width), bf16),
            pltpu.VMEM((tokens, split), bf16),
            pltpu.VMEM((tokens, split), bf16),
            pltpu.VMEM((tokens, split), bf16),
            pltpu.VMEM((tokens, split), bf16),
            pltpu.VMEM((tokens, width), bf16),
            pltpu.VMEM((tokens, split), bf16),
            pltpu.VMEM((tokens, split), bf16),
            pltpu.VMEM((2, depth * n, ff), bf16),
            pltpu.VMEM((deep * n, width), bf16),
            dma((n,)), dma((n,)), dma((n,)), dma((n,)),
            dma((2 * outer, 2)), dma((2 * outer, 2)),
            dma((outer, 2)), dma((outer, 2)),
            dma((2 * outer, 2)), dma((2 * outer, 2)),
            dma((4 * outer, 2)), dma((4 * outer, 2)),
        ],
        compiler_params=pltpu.CompilerParams(
            collective_id=0, has_side_effects=True, vmem_limit_bytes=56 * 1024 * 1024
        ),
    )(
        inputs, col_list.reshape(1, length), row_list.reshape(1, length), gain_attn.reshape(1, width), w_qkv, w_out,
        gain_ffn.reshape(1, width), w_gate, w_up, w_down,
    )
    return result.reshape(rows_here, length, width)


def solution(mesh):
    placed = (
        P("sample", "harm", None),
        P("sample"),
        P("sample"),
        P(),
        P(),
        P(),
        P(),
        P("harm", None),
        P("harm", None),
        P("harm", None),
    )
    return jax.shard_map(
        functools.partial(per_device, mesh.shape["harm"]),
        mesh=mesh, in_specs=placed, out_specs=P("harm", "sample", None), check_vma=False,
    )
```

```python
import functools

import jax
import jax.numpy as jnp
from jax import lax
from jax.experimental import pallas as pl
from jax.experimental.pallas import tpu as pltpu
from jax.sharding import PartitionSpec as P

HEADS = 8
WIN = 256
MESH = pl.DeviceIdType.MESH

eps = 1e-06
masked = -1e30


def rms_scale(values, gain):
    values = values.astype(jnp.float32)
    mean_sq = jnp.mean(values * values, axis=-1, keepdims=True)
    return values * lax.rsqrt(mean_sq + eps) * gain


def dot(a, b):
    return jnp.dot(a, b, preferred_element_type=jnp.float32)


def one_hot_rows(index, size):
    lanes = lax.broadcasted_iota(jnp.int32, (index.shape[0], size), 1)
    return jnp.where(lanes == index, 1.0, 0.0).astype(jnp.bfloat16)


def attention(query, key_ref, value_ref, start, width, allowed, scale, pair):
    low = lax.broadcasted_iota(jnp.int32, query.shape, 1) < pair // 2
    keys = key_ref[:, start : start + width]
    values = value_ref[:, start : start + width]
    zero = jnp.zeros_like(query)
    mixed = []
    for part in (jnp.where(low, query, zero), jnp.where(low, zero, query)):
        scores = lax.dot_general(part, keys, (((1,), (1,)), ((), ())), preferred_element_type=jnp.float32)
        scores = jnp.where(allowed, scores * scale, masked)
        top = jnp.max(scores, axis=-1, keepdims=True)
        weights = jnp.exp(scores - top)
        probs = (weights / jnp.sum(weights, axis=-1, keepdims=True)).astype(jnp.bfloat16)
        mixed.append(dot(probs, values))
    return jnp.where(low, mixed[0], mixed[1]).astype(jnp.bfloat16)


def kernel(
    n, x_ref, col_ref, row_ref, gain_a_ref, w_qkv_hbm, w_out_hbm, gain_f_ref, gate_ref, up_ref, down_ref,
    out_ref, w_qkv_ref, w_out_ref, w_sem, mc_ref, mr_ref, sent, ell_out, q_buf, k_buf, v_buf, got, got_ell, attn_m, gu, dn,
    sx_send, sx_recv, sa_send, sa_recv, z_send, z_recv, x_send, x_recv, y_send, y_recv, c_send, c_recv,
):
    me = lax.axis_index("harm")
    sample = lax.axis_index("sample")
    part = sample % 2
    other_plane = {"sample": sample + 1 - 2 * part, "harm": me}
    outer = n // 4
    zc, inner = me // 4, me % 4
    side, core = inner // 2, inner % 2
    other_side = {"harm": zc * 4 + (1 - side) * 2 + core}
    other_core = {"harm": zc * 4 + side * 2 + (1 - core)}
    depth = gate_ref.shape[0]
    deep = down_ref.shape[0]
    tokens, width = x_ref.shape[0] * x_ref.shape[1], x_ref.shape[2]
    block = tokens // n
    split = width // 2
    head_dim = width // HEADS
    pair = 2 * head_dim
    scale = head_dim ** (-0.5)
    step = min(tokens, 256)

    fetch_qkv = pltpu.make_async_copy(w_qkv_hbm, w_qkv_ref, w_sem.at[0])
    fetch_out = pltpu.make_async_copy(w_out_hbm, w_out_ref, w_sem.at[1])
    fetch_qkv.start()
    fetch_out.start()
    barrier = pltpu.get_barrier_semaphore()
    for d in range(1, n):
        pl.semaphore_signal(barrier, inc=1, device_id={"harm": (me + d) % n}, device_id_type=MESH)
    pl.semaphore_signal(barrier, inc=1, device_id=other_plane, device_id_type=MESH)

    length = col_ref.shape[1]
    cols, rows_here = tokens // length, length // n
    low_bits, mid_bits = cols.bit_length() - 1, rows_here.bit_length() - 1
    wide = lax.broadcasted_iota(jnp.int32, (length, length), 1)
    tall = lax.broadcasted_iota(jnp.int32, (length, length), 0)

    def upright(ref):
        return jnp.sum(jnp.where(wide == tall, ref[...].astype(jnp.float32), 0.0), axis=1, keepdims=True)

    def slots(shape, axis):
        t = lax.broadcasted_iota(jnp.int32, shape, axis)
        c = t & (cols - 1)
        source = t >> (low_bits + mid_bits)
        row = (t >> low_bits) & (rows_here - 1)
        return [t >> low_bits, me * cols + c, me * rows_here + row, source * cols + c]

    def fields(axis):
        shape = (tokens, length) if axis == 0 else (length, tokens)
        lists = (row_ref, col_ref, row_ref, col_ref)
        which = lax.broadcasted_iota(jnp.int32, shape, 1 - axis)
        out = []
        for ref, slot in zip(lists, slots(shape, axis)):
            values = ref[...].astype(jnp.float32) if axis == 0 else upright(ref)
            picked = jnp.where(which == slot, values, 0.0)
            out.append(jnp.sum(picked, axis=1 - axis, keepdims=True).astype(jnp.int32))
        return out

    for k, value in enumerate(fields(0)):
        mc_ref[:, k + 1 : k + 2] = value
    for k, value in enumerate(fields(1)):
        mr_ref[k + 1 : k + 2, :] = value
    t = lax.broadcasted_iota(jnp.int32, (tokens, 1), 0)
    mc_ref[:, 0:1] = mc_ref[:, 1:2] * cols + (t & (cols - 1))
    in_row = t & (length - 1)
    source = in_row >> low_bits
    row = t >> (length.bit_length() - 1)
    mc_ref[:, 5:6] = (source << (low_bits + mid_bits)) + (row << low_bits) + (in_row & (cols - 1))

    gu[0, pl.ds(pl.multiple_of(me * depth, depth), depth), :] = gate_ref[...]
    gu[1, pl.ds(pl.multiple_of(me * depth, depth), depth), :] = up_ref[...]
    dn[pl.ds(pl.multiple_of(me * deep, deep), deep), :] = down_ref[...]
    sent[...] = dot(one_hot_rows(mc_ref[:, 0:1], tokens), x_ref[...].reshape(tokens, width)).astype(jnp.bfloat16)

    pl.semaphore_wait(barrier, n)

    def rows_of(ref, i):
        return ref.at[pl.ds(pl.multiple_of(i * block, block), block), :]

    def to_row(src, dst, send, recv, d):
        peer = (me + d) % n
        return pltpu.make_async_remote_copy(
            src_ref=rows_of(src, peer), dst_ref=rows_of(dst, me), send_sem=send.at[d], recv_sem=recv.at[d],
            device_id={"harm": peer}, device_id_type=MESH,
        )

    def pieces(i, halves, send, recv, slot, device):
        copies = []
        for k, ref in enumerate((gu, dn)):
            half = halves[k]
            if half is None:
                continue
            size = (depth, deep)[k]
            first, rows = i * size, size
            if half is not whole:
                rows = size // 2
                first = first + half * rows
            where = pl.ds(pl.multiple_of(first, rows), rows)
            piece = ref.at[:, where, :] if k == 0 else ref.at[where, :]
            copies.append(
                pltpu.make_async_remote_copy(
                    src_ref=piece, dst_ref=piece, send_sem=send.at[slot, k], recv_sem=recv.at[slot, k],
                    device_id=device, device_id_type=MESH,
                )
            )
        return copies

    whole = "all"
    full, mine, theirs = (whole, whole), (part, part), (1 - part, 1 - part)
    traded = (part, part)

    def place(z, s, c):
        return z * 4 + s * 2 + c

    pending = []

    def guard(cond, body):
        if cond is None:
            body()
        else:
            pl.when(cond)(body)

    def start(build, cond=None):
        def body():
            for copy in build():
                copy.start()

        guard(cond, body)
        pending.append((cond, build))

    def arrived(build, cond=None):
        def body():
            for copy in build():
                copy.wait_recv()

        guard(cond, body)

    def send(cond, *args):
        start(lambda: pieces(*args), cond)

    def receive(cond, *args):
        arrived(lambda: pieces(*args), cond)

    def both(a, b):
        return b if a is None else a & b

    def reached(t):
        if t == 0:
            return [(zc, None, 0)]
        return [(zc - t, zc - t >= 0, 0), (zc + t, zc + t < outer, 1)]

    def along_z(t, z, cond, stream):
        step_z = 1 - 2 * stream
        ahead = zc + step_z
        ok = both(cond, (ahead < outer) if stream == 0 else (ahead >= 0))
        if t + 1 < outer:
            device = {"harm": ahead * 4 + inner}
            send(ok, place(z, side, core), mine, z_send, z_recv, stream * outer + t + 1, device)

    def z_stage(t):
        for z, cond, stream in reached(t):
            i = place(z, side, core)
            receive(cond, i, mine, z_send, z_recv, stream * outer + t, other_core)
            along_z(t, z, cond, stream)
            send(cond, i, mine, x_send, x_recv, z, other_side)
            send(cond, i, traded, y_send, y_recv, z, other_plane)
            send(cond, i, mine, c_send, c_recv, z, other_core)

    def x_stage(t):
        for z, cond, stream in reached(t):
            i = place(z, 1 - side, core)
            receive(cond, i, mine, x_send, x_recv, z, other_side)
            send(cond, i, traded, y_send, y_recv, outer + z, other_plane)
            send(cond, i, mine, c_send, c_recv, outer + z, other_core)

    def y_stage(t, other):
        for z, cond, stream in reached(t):
            i = place(z, 1 - side if other else side, core)
            slot = outer * other + z
            receive(cond, i, theirs, y_send, y_recv, slot, other_plane)
            send(cond, i, theirs, c_send, c_recv, 2 * outer + slot, other_core)

    def core_stage(t, other, k):
        def only(halves):
            return tuple(half if j == k else None for j, half in enumerate(halves))

        for z, cond, stream in reached(t):
            i = place(z, 1 - side if other else side, 1 - core)
            slot = outer * other + z
            if t == 0 and not other:
                receive(None, i, only(full), c_send, c_recv, slot, other_core)
            else:
                receive(cond, i, only(mine), c_send, c_recv, slot, other_core)
                receive(cond, i, only(theirs), c_send, c_recv, 2 * outer + slot, other_core)

    def tokens_out(src, dst, send_sem, recv_sem):
        return lambda: [to_row(src, dst, send_sem, recv_sem, d) for d in range(1, n)]

    for stream in (0, 1):
        along_z(0, zc, None, stream)
    send(None, me, mine, x_send, x_recv, zc, other_side)
    send(None, me, full, c_send, c_recv, zc, other_core)
    start(tokens_out(sent, got, sx_send, sx_recv))
    rows_of(got, me)[...] = rows_of(sent, me)[...]

    def project(source, first):
        normed = rms_scale(source[...], gain_a_ref[...]).astype(jnp.bfloat16)
        for buf, base in ((q_buf, 0), (k_buf, width), (v_buf, 2 * width)):
            buf[...] = dot(normed, w_qkv_ref[:, base + first : base + first + split]).astype(jnp.bfloat16)

    def attend(dest, marks, level, along_ell):
        def body(i, carry):
            rows = pl.ds(pl.multiple_of(i * step, step), step)
            ell_q, col_q = mc_ref[rows, level : level + 1], mc_ref[rows, marks : marks + 1]
            ell_k, col_k = mr_ref[level : level + 1, :], mr_ref[marks : marks + 1, :]
            if along_ell:
                same, diff = col_q == col_k, ell_k - ell_q
            else:
                same, diff = ell_q == ell_k, col_k - col_q
            allowed = same & (diff >= -(WIN // 2)) & (diff < WIN // 2) & (ell_k >= col_k)
            for p in range(split // pair):
                query = q_buf[rows, p * pair : (p + 1) * pair]
                dest[rows, p * pair : (p + 1) * pair] = attention(
                    query, k_buf, v_buf, p * pair, pair, allowed, scale, pair
                )
            return carry

        lax.fori_loop(0, tokens // step, body, 0)

    fetch_qkv.wait()
    project(sent, 0)
    z_stage(1)
    attend(ell_out, 2, 1, True)
    start(tokens_out(ell_out, got_ell, sa_send, sa_recv))
    rows_of(got_ell, me)[...] = rows_of(ell_out, me)[...]

    x_stage(0)
    for t in range(2, outer):
        z_stage(t)
        x_stage(t - 1)
    y_stage(0, 1)
    arrived(tokens_out(sent, got, sx_send, sx_recv))
    project(got, split)
    x_stage(outer - 1)
    attend(attn_m, 4, 3, False)
    for t in range(1, outer):
        y_stage(t, 0)
        y_stage(t, 1)

    arrived(tokens_out(ell_out, got_ell, sa_send, sa_recv))
    fetch_out.wait()
    resid = got[...].astype(jnp.float32) + (
        dot(got_ell[...], w_out_ref[:split, :]) + dot(attn_m[...], w_out_ref[split:, :])
    )
    normed_ffn = rms_scale(resid, gain_f_ref[...]).astype(jnp.bfloat16)

    for t in range(outer):
        for other in (0, 1):
            core_stage(t, other, 0)
    gate = dot(normed_ffn, gu[0])
    up = dot(normed_ffn, gu[1])
    hidden = (gate / (1.0 + jnp.exp(-gate)) * up).astype(jnp.bfloat16)
    for t in range(outer):
        for other in (0, 1):
            core_stage(t, other, 1)
    final = resid + dot(hidden, dn[...])
    valid = mc_ref[:, 4:5] <= mc_ref[:, 3:4]
    final = jnp.where(valid, final, 0.0).astype(jnp.bfloat16)
    out_ref[...] = dot(one_hot_rows(mc_ref[:, 5:6], tokens), final).astype(jnp.bfloat16)
    for cond, build in pending:

        def finish(build=build):
            for copy in build():
                copy.wait_send()

        guard(cond, finish)


def per_device(n, inputs, col_list, row_list, gain_attn, w_qkv, w_out, gain_ffn, w_gate, w_up, w_down):
    length, cols, width = inputs.shape
    rows_here = length // n
    tokens = length * cols
    split = width // 2
    bf16 = jnp.bfloat16
    depth, ff = w_gate.shape
    deep = w_down.shape[0]
    outer = n // 4
    vmem = pl.BlockSpec(memory_space=pltpu.VMEM)
    hbm = pl.BlockSpec(memory_space=pl.ANY)
    dma = pltpu.SemaphoreType.DMA
    result = pl.pallas_call(
        functools.partial(kernel, n),
        out_shape=jax.ShapeDtypeStruct((tokens, width), bf16),
        in_specs=[vmem] * 4 + [hbm] * 2 + [vmem] * 4,
        out_specs=vmem,
        scratch_shapes=[
            pltpu.VMEM(w_qkv.shape, bf16),
            pltpu.VMEM(w_out.shape, bf16),
            dma((2,)),
            pltpu.VMEM((tokens, 8), jnp.int32),
            pltpu.VMEM((8, tokens), jnp.int32),
            pltpu.VMEM((tokens, width), bf16),
            pltpu.VMEM((tokens, split), bf16),
            pltpu.VMEM((tokens, split), bf16),
            pltpu.VMEM((tokens, split), bf16),
            pltpu.VMEM((tokens, split), bf16),
            pltpu.VMEM((tokens, width), bf16),
            pltpu.VMEM((tokens, split), bf16),
            pltpu.VMEM((tokens, split), bf16),
            pltpu.VMEM((2, depth * n, ff), bf16),
            pltpu.VMEM((deep * n, width), bf16),
            dma((n,)), dma((n,)), dma((n,)), dma((n,)),
            dma((2 * outer, 2)), dma((2 * outer, 2)),
            dma((outer, 2)), dma((outer, 2)),
            dma((2 * outer, 2)), dma((2 * outer, 2)),
            dma((4 * outer, 2)), dma((4 * outer, 2)),
        ],
        compiler_params=pltpu.CompilerParams(
            collective_id=0, has_side_effects=True, vmem_limit_bytes=56 * 1024 * 1024
        ),
    )(
        inputs, col_list.reshape(1, length), row_list.reshape(1, length), gain_attn.reshape(1, width), w_qkv, w_out,
        gain_ffn.reshape(1, width), w_gate, w_up, w_down,
    )
    return result.reshape(rows_here, length, width)


def solution(mesh):
    placed = (
        P("sample", "harm", None),
        P("sample"),
        P("sample"),
        P(),
        P(),
        P(),
        P(),
        P("harm", None),
        P("harm", None),
        P("harm", None),
    )
    return jax.shard_map(
        functools.partial(per_device, mesh.shape["harm"]),
        mesh=mesh, in_specs=placed, out_specs=P("harm", "sample", None), check_vma=False,
    )
```
